256 devices in a mesh: expert: 32 (over x, z), vocab: 8 (over y, core).
Axes of the slice: x: 4, y: 4, z: 8, core: 2. Of those that a mesh axis runs over, the one named last changes fastest.
Arguments:
- out_grad: bfloat16 [4096, 4096], P('expert', 'vocab'), may hold values from -6 to 6
- residual_stream: bfloat16 [4096, 4096], P('expert', 'vocab'), may hold values from -228 to 228
- norm_gain: float32 [4096], P('vocab'), may hold values from 0.25 to 51
- expert_ids: int32 [4096, 8], P('expert'), may hold values from 0 to 31, all different within a row; in each aligned block of 128 rows (0 to 127, 128 to 255, ...) at most 38 rows name the same one
- gate_scores: float32 [4096, 8], P('expert'), may hold values from 0.05 to 1
- saved_gate: bfloat16 [32, 1216, 1536], P('expert', None, 'vocab'), may hold values from -6 to 6
- saved_up: bfloat16 [32, 1216, 1536], P('expert', None, 'vocab'), may hold values from -6 to 6
- gate_weight: bfloat16 [32, 4096, 1536], P('expert', None, 'vocab'), may hold values from -0.09375 to 0.09375
- up_weight: bfloat16 [32, 4096, 1536], P('expert', None, 'vocab'), may hold values from -0.09375 to 0.09375
- down_weight: bfloat16 [32, 1536, 4096], P('expert', 'vocab'), may hold values from -0.15625 to 0.15625
- embedding: bfloat16 [98304, 4096], P(('expert', 'vocab')), may hold values from -0.09375 to 0.09375
- allowed: int32 [98304], P(('expert', 'vocab')), may hold values 0 or 1
- suffix_start: int32 [32], P('expert'), may hold values from 0 to 108
Outputs:
- token_grad: bfloat16 [4096, 4096], P('expert', 'vocab')
- scores: float32 [640, 98304], P(None, ('expert', 'vocab'))
The draws below stay inside these ranges and needn't reach their ends.
Inputs may be any that keep to these rules, and one draw needn't show every extreme that they name: `expert_ids`: in each aligned block of 128 rows (one behavior) a row names 8 different experts and no expert is named by more than 38 rows; some expert is named by exactly 38 rows in some blocks.
All inputs are finite; a program needn't handle non-finite values. No bound on the sum of `allowed` on one device may be relied on, other than what follows from the above.
Results may differ from the reference program's by a relative error of at most 0.01.
Values may be sent and summed in bfloat16 or wider, within the bound.
No kernel may reach another device: no remote copies, remote signals or barrier semaphores. Data moves between devices by JAX's collectives and lax.ppermute only.
A program may use at most 128 MiB of HBM per device.

```python
import math
import jax
import jax.numpy as jnp
import numpy as np
from jax import lax

D = 4096
FF = 1536
TOP = 8
SEQ = 128
SUFFIX = 20
EXPERTS = 32
BEHAVIORS = 32
TOKENS = 4096
CAP = 38
SLOTS = 1216
VOCAB = 98304
N_EXPERT = 32
N_VOCAB = 8


massive_count = 4


def massive_mask(key):
    order = jax.random.permutation(jax.random.fold_in(key, 101), D)
    picked = order[:massive_count]
    return jnp.zeros((D,), jnp.float32).at[picked].set(1.0) > 0.5


def draw_residual_stream(key, part):
    key_base, key_rows, key_big, key_sign = jax.random.split(jax.random.fold_in(key, 7), 4)
    columns = jnp.exp(math.log(3.0) * jnp.arange(D, dtype=jnp.float32) / D)
    base = jnp.clip(jax.random.normal(key_base, (TOKENS, D), jnp.float32), -5.0, 5.0)
    bulk = base * columns[None, :]
    amplitude = jnp.sqrt(jnp.mean(columns * columns) * D / massive_count)
    magnitude = jax.random.uniform(key_big, (TOKENS, D), jnp.float32, 0.7, 1.4)
    signs = jnp.where(jax.random.bernoulli(key_sign, 0.5, (TOKENS, D)), 1.0, -1.0)
    strong = amplitude * magnitude * signs
    mask = massive_mask(key)
    values = jnp.where(mask[None, :], strong, bulk)
    row_scale = jnp.exp(jax.random.uniform(key_rows, (TOKENS, 1), jnp.float32, math.log(0.1), math.log(1.0)))
    return (values * row_scale).astype(jnp.bfloat16)


def draw_norm_gain(key, part):
    key_base, key_big = jax.random.split(jax.random.fold_in(key, 13))
    base = 1.0 + 0.18 * jnp.clip(jax.random.normal(key_base, (D,), jnp.float32), -4.0, 4.0)
    strong = jnp.sqrt(jnp.float32(D) / massive_count) * jax.random.uniform(key_big, (D,), jnp.float32, 0.7, 1.4)
    mask = massive_mask(key)
    return jnp.where(mask, strong, base).astype(jnp.float32)


def touch_ends(entries, rng, low, top_value):
    dims = entries.shape
    place = [jax.random.randint(jax.random.fold_in(rng, axis), (), 0, dims[axis]) for axis in range(len(dims))]
    entries = entries.at[tuple(place)].set(low)
    longest = dims.index(max(dims))
    place[longest] = (place[longest] + 1) % dims[longest]
    return entries.at[tuple(place)].set(top_value)


def level_of(stream_key, extent, cuts, smallest, top_value):
    factor_of = 1.0
    for axis_at, blocks in cuts:
        steps = jax.random.uniform(jax.random.fold_in(jax.random.fold_in(stream_key, 6), axis_at), (blocks,), jnp.float32, smallest / len(cuts), top_value / len(cuts))
        factor_of = factor_of * jnp.repeat(jnp.exp(steps), extent[axis_at] // blocks).reshape((-1,) + (1,) * (len(extent) - 1 - axis_at))
    return factor_of


def deal_out(rng, own, number, rows, count, top, bound, slope):
    sequence = jax.random.permutation(rng, count)
    packed, common = load_shares(count, rows * top, bound, slope, True), load_shares(count, rows * top, bound, slope, False)
    places = jnp.arange(count)

    def named(tallies, offset_by):
        used = int((tallies > 0).sum())
        fixed = max(1, used // 4)
        shifted = fixed + (places - fixed + offset_by * (used - fixed)) % max(1, count - fixed)
        return jnp.zeros((count,), jnp.int32).at[sequence[jnp.where(places < fixed, places, shifted)]].set(jnp.asarray(tallies, jnp.int32))

    tallies = jnp.where(number % 4 == 0, named(packed, number // 4), named(common, number - number // 4 - 1))
    mixed = jax.random.permutation(jax.random.fold_in(own, 3), count)
    source_of, receiver = mixed[0:count // 2 * 2:2], mixed[1:count // 2 * 2:2]
    room = jnp.minimum(tallies[source_of] - 1, bound - tallies[receiver]) // 2
    room = jnp.where((source_of == sequence[0]) | (receiver == sequence[0]) | (tallies[receiver] == 0), 0, jnp.maximum(room, 0))
    shifted = jax.random.randint(jax.random.fold_in(own, 4), (count // 2,), 0, 1 << 20) % (room + 1)
    tallies = tallies.at[source_of].add(-shifted).at[receiver].add(shifted)
    items = jnp.searchsorted(jnp.cumsum(tallies), jnp.arange(rows * top), side="right").astype(jnp.int32)
    listing = items.reshape(top, rows).T
    listing = listing[jax.random.permutation(jax.random.fold_in(own, 1), rows)]
    offset_by = jax.random.randint(jax.random.fold_in(own, 2), (rows, 1), 0, top)
    return jnp.take_along_axis(listing, (jnp.arange(top)[None, :] + offset_by) % top, axis=1)


def load_shares(number_of, total, most, skew, full):
    weights = [(1 << 20) // math.isqrt(standing ** skew) + 1 for standing in range(1, number_of + 1)]
    largest = most if full else min(most, max(-(-total // number_of), total * weights[0] // sum(weights)))
    least = 1 if total - largest >= number_of - 1 else 0
    given, spare = [largest] + [least] * (number_of - 1), total - largest - least * (number_of - 1)
    while spare > 0:
        candidates = [i for i in range(1, number_of) if given[i] < largest] or [i for i in range(1, number_of) if given[i] < most]
        pool, left = sum([weights[i] for i in candidates]), spare
        for i in candidates:
            more = min(most - given[i], max(1, left * weights[i] // pool), spare)
            given[i] = given[i] + more
            spare = spare - more
    return np.array(given)


def gaussian(own_key, shape, width, bound, cuts=(), kind=jnp.bfloat16):
    loudness = level_of(own_key, shape, cuts, -0.22, 0.18) if cuts else 1.0
    entries = jax.random.normal(own_key, shape, jnp.float32) * width * loudness
    return jnp.minimum(jnp.maximum(entries, -bound), bound).astype(kind)


def setup_inputs(seed: int = 0) -> dict:
    key_of = jax.random.split(jax.random.key(seed), 14)
    out_grad = gaussian(key_of[0], (TOKENS, D), 1.0, 6.0, ((0, 32), (1, 8)))
    residual_stream = draw_residual_stream(jax.random.fold_in(key_of[13], 71), 0)
    norm_gain = draw_norm_gain(jax.random.fold_in(key_of[13], 71), 0)
    expert_ids_keys = jax.random.split(jax.random.fold_in(key_of[3], 1), TOKENS // SEQ)
    expert_ids_turns = jax.random.permutation(jax.random.fold_in(key_of[3], 3), TOKENS // SEQ)
    expert_ids = jax.vmap(lambda own, number: deal_out(jax.random.fold_in(key_of[3], 2), own, number, SEQ, EXPERTS, TOP, CAP, 2))(expert_ids_keys, expert_ids_turns).reshape((TOKENS, TOP))
    gate_scores = jnp.clip(jnp.exp(math.log(1.0) - 2.9957323 * jax.random.uniform(key_of[4], (TOKENS, TOP), jnp.float32) ** level_of(key_of[4], (TOKENS, TOP), ((0, 32),), -0.2, 0.2)), 0.05, 1.0)
    saved_gate = gaussian(key_of[5], (EXPERTS, SLOTS, FF), 1.0, 6.0, ((0, 32), (2, 8)))
    saved_up = gaussian(key_of[6], (EXPERTS, SLOTS, FF), 1.0, 6.0, ((0, 32), (2, 8)))
    gate_weight = gaussian(key_of[7], (EXPERTS, D, FF), D ** -0.5, 0.09375, ((0, 32), (2, 8)))
    up_weight = gaussian(key_of[8], (EXPERTS, D, FF), D ** -0.5, 0.09375, ((0, 32), (2, 8)))
    down_weight = gaussian(key_of[9], (EXPERTS, FF, D), FF ** -0.5, 0.15625, ((0, 32), (1, 8)))
    embedding = gaussian(key_of[10], (VOCAB, D), D ** -0.5, 0.09375, ((0, 256),))
    allowed = touch_ends((jax.random.randint(key_of[11], (VOCAB,), 0, 4) < 3).astype(jnp.int32), jax.random.fold_in(key_of[11], 1), 0, 1)
    suffix_start = touch_ends(jax.random.randint(key_of[12], (BEHAVIORS,), 0, SEQ - SUFFIX + 1), jax.random.fold_in(key_of[12], 1), 0, SEQ - SUFFIX).astype(jnp.int32)
    return dict(out_grad=out_grad, residual_stream=residual_stream, norm_gain=norm_gain, expert_ids=expert_ids, gate_scores=gate_scores, saved_gate=saved_gate, saved_up=saved_up, gate_weight=gate_weight, up_weight=up_weight, down_weight=down_weight, embedding=embedding, allowed=allowed, suffix_start=suffix_start)


def slot_places(expert_ids):
    blocks = expert_ids.reshape(N_EXPERT, SEQ * TOP)
    matches = (blocks[:, :, None] == jnp.arange(EXPERTS, dtype=jnp.int32)[None, None, :]).astype(jnp.int32)
    before = jnp.cumsum(matches, axis=1) - matches
    position = lax.optimization_barrier(jnp.sum(before * matches, axis=2)).astype(jnp.int32)
    source = jnp.arange(N_EXPERT, dtype=jnp.int32)[:, None]
    slot = (source * CAP + position).astype(jnp.int32)
    return (blocks.reshape(-1), slot.reshape(-1))

def reference(out_grad, residual_stream, norm_gain, expert_ids, gate_scores, saved_gate, saved_up, gate_weight, up_weight, down_weight, embedding, allowed, suffix_start):
    gate_share = gate_scores / lax.optimization_barrier(jnp.sum(gate_scores, axis=1, keepdims=True))
    chosen, slot = slot_places(expert_ids)
    token_of = (jnp.arange(TOKENS * TOP, dtype=jnp.int32) // TOP).astype(jnp.int32)
    owner = jnp.full((EXPERTS, SLOTS), TOKENS, jnp.int32).at[chosen, slot].set(token_of)
    share_of = jnp.zeros((EXPERTS, SLOTS), jnp.float32).at[chosen, slot].set(gate_share.reshape(-1))
    grad_ext = jnp.concatenate([out_grad.astype(jnp.float32), jnp.zeros((1, D), jnp.float32)], axis=0)
    group = FF // N_VOCAB

    def expert_step(accumulated, pieces):
        rows, slot_gate, pre_gate, pre_up, w_gate, w_up, w_down = pieces
        routed = (slot_gate[:, None] * grad_ext[rows]).astype(jnp.bfloat16)
        act_grad = jnp.dot(routed, w_down.T, preferred_element_type=jnp.float32)
        pre_gate = pre_gate.astype(jnp.float32)
        pre_up = pre_up.astype(jnp.float32)
        sigmoid_g = jax.nn.sigmoid(pre_gate)
        gate_grad = (act_grad * pre_up * sigmoid_g * (1.0 + pre_gate * (1.0 - sigmoid_g))).astype(jnp.bfloat16)
        up_grad = (act_grad * pre_gate * sigmoid_g).astype(jnp.bfloat16)
        gate_split = gate_grad.astype(jnp.float32).reshape(SLOTS, N_VOCAB, group)
        up_split = up_grad.astype(jnp.float32).reshape(SLOTS, N_VOCAB, group)
        wg_split = w_gate.astype(jnp.float32).reshape(D, N_VOCAB, group)
        wu_split = w_up.astype(jnp.float32).reshape(D, N_VOCAB, group)
        partial_value = jnp.einsum('rvh,dvh->vrd', gate_split, wg_split) + jnp.einsum('rvh,dvh->vrd', up_split, wu_split)
        rounded = lax.optimization_barrier(partial_value.astype(jnp.bfloat16))
        slot_grad = lax.optimization_barrier(jnp.sum(rounded.astype(jnp.float32), axis=0))
        accumulated = accumulated.at[rows].add(slot_grad, mode='drop')
        return (accumulated, None)
    moe_grad, _ = lax.scan(expert_step, jnp.zeros((TOKENS, D), jnp.float32), (owner, share_of, saved_gate, saved_up, gate_weight, up_weight, down_weight))
    resid = residual_stream.astype(jnp.float32)
    inverse = lax.rsqrt(lax.optimization_barrier(jnp.mean(resid * resid, axis=1)) + 1e-06)
    normed = resid * inverse[:, None]
    scaled = moe_grad * norm_gain[None, :]
    project = lax.optimization_barrier(jnp.mean(scaled * normed, axis=1))
    token_grad = (out_grad.astype(jnp.float32) + inverse[:, None] * (scaled - normed * project[:, None])).astype(jnp.bfloat16)
    per_behavior = token_grad.reshape(N_EXPERT, SEQ, D)

    def take_suffix(rows, first_row):
        return lax.dynamic_slice_in_dim(rows, first_row.astype(jnp.int32), SUFFIX, 0)
    suffix_grad = jax.vmap(take_suffix)(per_behavior, suffix_start).reshape(N_EXPERT * SUFFIX, D)
    raw_scores = -jnp.dot(suffix_grad, embedding.T, preferred_element_type=jnp.float32)
    scores = jnp.where(allowed[None, :] > 0, raw_scores, jnp.float32(0.0))
    return (token_grad, scores)
```

```python
import functools

import jax
import jax.numpy as jnp
from jax import lax
from jax.experimental import pallas as pl
from jax.experimental.pallas import tpu as pltpu
from jax.sharding import PartitionSpec as P


D = 4096
SUFFIX = 20
PAD = 40
SLICE = 512
HID = 192
CHUNKS = ((0, 24), (24, 16))
TILE = 160
NT = (((1,), (1,)), ((), ()))
NN = (((1,), (0,)), ((), ()))


def shifted(value, by):
    n = lax.axis_size("vocab")
    return lax.ppermute(value, "vocab", [(i, (i + 2 * by) % n) for i in range(n)])


def swapped(value):
    n = lax.axis_size("vocab")
    return lax.ppermute(value, "vocab", [(i, i ^ 1) for i in range(n)])


def summed(value):
    n = lax.axis_size("vocab")
    parts = lax.all_to_all(
        jnp.broadcast_to(value[None], (n, *value.shape)), "vocab", 0, 0, tiled=True
    )
    return jnp.sum(parts, axis=0)


def dot(a, b, dims):
    return lax.dot_general(a, b, dims, preferred_element_type=jnp.float32)


def tiles(rows, width):
    return pl.BlockSpec((rows // 2, width), lambda i, *_: (i, 0))


def half_tiles(rows, width):
    return pl.BlockSpec((rows // 2, width), lambda i, core: (2 * core[0] + i, 0))


def const(shape, *index):
    return pl.BlockSpec(shape, lambda i, *_: index)


def params():
    return pltpu.CompilerParams(dimension_semantics=("arbitrary",))


def act_body(xo, xx, t0, t1, t2, t3, s0, s1, s2, s3, a0, a1, a2, a3):
    mine, other = xo[...], xx[...]
    for t, s, a in ((t0, s0, a0), (t1, s1, a1), (t2, s2, a2), (t3, s3, a3)):
        own = dot(mine, t[:, :SLICE], NT) + dot(other, t[:, SLICE:], NT)
        oth = dot(mine, s[:, SLICE:], NT) + dot(other, s[:, :SLICE], NT)
        a[:, :HID] = own.astype(jnp.bfloat16)
        a[:, HID:] = oth.astype(jnp.bfloat16)


def act_partials(mine, other, own_w, other_w):
    rows = other.shape[0]
    return pl.pallas_call(
        act_body,
        grid=(2,),
        in_specs=[tiles(rows, SLICE)] * 2 + [const((HID, 2 * SLICE), 0, 0)] * 8,
        out_specs=[tiles(rows, 2 * HID)] * 4,
        out_shape=[jax.ShapeDtypeStruct((rows, 2 * HID), jnp.bfloat16)] * 4,
        compiler_params=params(),
        cost_estimate=pl.CostEstimate(
            flops=2 * rows * 2 * SLICE * 8 * HID, bytes_accessed=6_000_000, transcendentals=0
        ),
        name="act_partials",
    )(mine, other, *own_w, *other_w)


def gated_body(a0, a1, a2, a3, saved, top, bottom):
    act = (a0[...].astype(jnp.float32) + a1[...].astype(jnp.float32)) + (
        a2[...].astype(jnp.float32) + a3[...].astype(jnp.float32)
    )

    def store(out):
        for at in (0, 1):
            a = act[:, at * HID : (at + 1) * HID]
            base = 2 * at * HID
            g = saved[:, base : base + HID].astype(jnp.float32)
            u = saved[:, base + HID : base + 2 * HID].astype(jnp.float32)
            s = jax.nn.sigmoid(g)
            out[:, base : base + HID] = (a * u * s * (1.0 + g * (1.0 - s))).astype(jnp.bfloat16)
            out[:, base + HID : base + 2 * HID] = (a * g * s).astype(jnp.bfloat16)

    pl.when(pl.program_id(0) == 0)(lambda: store(top))
    pl.when(pl.program_id(0) == 1)(lambda: store(bottom))


def gated(parts, saved):
    rows = saved.shape[0]
    return pl.pallas_call(
        gated_body,
        grid=(2,),
        in_specs=[tiles(rows, 2 * HID)] * 4 + [tiles(rows, 4 * HID)],
        out_specs=[const((rows // 2, 4 * HID), 0, 0)] * 2,
        out_shape=[jax.ShapeDtypeStruct((rows // 2, 4 * HID), jnp.bfloat16)] * 2,
        compiler_params=params(),
        cost_estimate=pl.CostEstimate(
            flops=rows * 2 * HID * 20, bytes_accessed=3_000_000, transcendentals=rows * 2 * HID
        ),
        name="gated",
    )(*parts, saved)


def back_body(n, *refs):
    tops, bottoms = refs[:n], refs[n : 2 * n]
    own_w, other_w = refs[2 * n : 3 * n], refs[3 * n : 4 * n]
    out_own, out_oth = refs[4 * n :]
    upper = pl.program_id(0) == 0
    own = oth = None
    for top, bottom, t, s in zip(tops, bottoms, own_w, other_w):
        b = jnp.where(upper, top[...], bottom[...])
        left, right = b[:, : 2 * HID], b[:, 2 * HID :]
        o = dot(left, t[:, :SLICE], NN) + dot(right, s[:, SLICE:], NN)
        x = dot(left, t[:, SLICE:], NN) + dot(right, s[:, :SLICE], NN)
        own = o if own is None else own + o
        oth = x if oth is None else oth + x
    out_own[...] = own
    out_oth[...] = oth


def back_first(blocks, own_w, other_w):
    rows, n = 2 * blocks[0][0].shape[0], len(blocks)
    return pl.pallas_call(
        functools.partial(back_body, n),
        grid=(2,),
        in_specs=[const((rows // 2, 4 * HID), 0, 0)] * (2 * n)
        + [const((2 * HID, 2 * SLICE), 0, 0)] * (2 * n),
        out_specs=[tiles(rows, SLICE)] * 2,
        out_shape=[jax.ShapeDtypeStruct((rows, SLICE), jnp.float32)] * 2,
        compiler_params=params(),
        cost_estimate=pl.CostEstimate(
            flops=2 * rows * 2 * SLICE * 4 * HID * n, bytes_accessed=9_000_000, transcendentals=0
        ),
        name="back_first",
    )(*[b[0] for b in blocks], *[b[1] for b in blocks], *own_w, *other_w)


def last_body(core, top, bottom, t, s, acc_own, acc_oth, out_own, out_oth):
    b = jnp.where(pl.program_id(0) == 0, top[...], bottom[...])
    left, right = b[:, : 2 * HID], b[:, 2 * HID :]
    own = acc_own[...] + dot(left, t[:, :SLICE], NN) + dot(right, s[:, SLICE:], NN)
    oth = acc_oth[...] + dot(left, t[:, SLICE:], NN) + dot(right, s[:, :SLICE], NN)
    out_own[...] = own.astype(jnp.bfloat16)
    out_oth[...] = oth.astype(jnp.bfloat16)


def back_last(core, top, bottom, t, s, acc_own, acc_oth):
    rows = acc_own.shape[0]
    return pl.pallas_call(
        last_body,
        grid_spec=pltpu.PrefetchScalarGridSpec(
            num_scalar_prefetch=1,
            grid=(2,),
            in_specs=[const((rows // 2, 4 * HID), 0, 0)] * 2
            + [const((2 * HID, 2 * SLICE), 0, 0)] * 2
            + [tiles(rows, SLICE)] * 2,
            out_specs=[half_tiles(rows, SLICE), tiles(rows, SLICE)],
        ),
        out_shape=[
            jax.ShapeDtypeStruct((2 * rows, SLICE), jnp.bfloat16),
            jax.ShapeDtypeStruct((rows, SLICE), jnp.bfloat16),
        ],
        compiler_params=params(),
        cost_estimate=pl.CostEstimate(
            flops=2 * rows * 2 * SLICE * 4 * HID, bytes_accessed=5_000_000, transcendentals=0
        ),
        name="back_last",
    )(core, top, bottom, t, s, acc_own, acc_oth)


def score_specs(blocks, words, rows):
    half = rows // TILE // 2
    top = pl.BlockSpec((TILE, SLICE), lambda i, at: (jnp.minimum(i, half - 1), 0))
    bottom = pl.BlockSpec((TILE, SLICE), lambda i, at: (jnp.maximum(i - half, 0), 0))
    tables = [
        pl.BlockSpec((words, SLICE), lambda i, at, j=j: (0, at[j])) for j in range(len(blocks))
    ]
    return [top, bottom] * len(blocks) + tables


def score_total(half, refs, n):
    upper = pl.program_id(0) < half
    total = None
    for j in range(n):
        block = jnp.where(upper, refs[2 * j][...], refs[2 * j + 1][...])
        one = dot(block, refs[2 * n + j][...], NT)
        total = one if total is None else total + one
    return total


def score_body(n, half, at, *refs):
    refs[-1][...] = score_total(half, refs, n)


def score_first(blocks, at, table):
    n, rows, words = len(blocks), 2 * blocks[0][0].shape[0], table.shape[0]
    return pl.pallas_call(
        functools.partial(score_body, n, rows // TILE // 2),
        grid_spec=pltpu.PrefetchScalarGridSpec(
            num_scalar_prefetch=1,
            grid=(rows // TILE,),
            in_specs=score_specs(blocks, words, rows),
            out_specs=pl.BlockSpec((TILE, words), lambda i, at: (i, 0)),
        ),
        out_shape=jax.ShapeDtypeStruct((rows, words), jnp.float32),
        compiler_params=params(),
        cost_estimate=pl.CostEstimate(
            flops=2 * rows * words * SLICE * n, bytes_accessed=8_000_000, transcendentals=0
        ),
        name="score_first",
    )(at, *[part for b in blocks for part in b], *[table] * n)


def score_last_body(n, half, at, *refs):
    acc, allowed, out = refs[3 * n :]
    total = acc[...] + score_total(half, refs, n)
    out[...] = jnp.where(allowed[...] > 0, -total, 0.0)


def score_last(blocks, at, table, acc, allowed):
    n, (rows, words) = len(blocks), acc.shape
    return pl.pallas_call(
        functools.partial(score_last_body, n, rows // TILE // 2),
        grid_spec=pltpu.PrefetchScalarGridSpec(
            num_scalar_prefetch=1,
            grid=(rows // TILE,),
            in_specs=score_specs(blocks, words, rows)
            + [
                pl.BlockSpec((TILE, words), lambda i, at: (i, 0)),
                pl.BlockSpec((1, words), lambda i, at: (0, 0)),
            ],
            out_specs=pl.BlockSpec((TILE, words), lambda i, at: (i, 0)),
        ),
        out_shape=jax.ShapeDtypeStruct((rows, words), jnp.float32),
        compiler_params=params(),
        cost_estimate=pl.CostEstimate(
            flops=4 * rows * words * SLICE, bytes_accessed=6_000_000, transcendentals=0
        ),
        name="score_last",
    )(at, *[part for b in blocks for part in b], *[table] * n, acc, allowed.reshape(1, words))


def shards(
    out_grad,
    residual_stream,
    norm_gain,
    expert_ids,
    gate_scores,
    saved_gate,
    saved_up,
    gate_weight,
    up_weight,
    down_weight,
    embedding,
    allowed,
    suffix_start,
):
    n_expert = lax.axis_size("expert")
    seq_len = out_grad.shape[0]
    slot_count = saved_gate.shape[1]
    capacity = slot_count // n_expert
    v = lax.axis_index("vocab")
    y, c = v // 2, v % 2
    half = n_expert // 2

    core = c.astype(jnp.int32).reshape(1)
    token = jnp.arange(seq_len, dtype=jnp.int32)

    def piece(weights, k):
        to = (y + k) % 4 * (2 * SLICE)
        own, oth = to + c * SLICE, to + (1 - c) * SLICE
        return jnp.concatenate(
            [
                jnp.concatenate(
                    [lax.dynamic_slice_in_dim(w, at, SLICE, 1) for w in weights], axis=0
                )
                for at in (own, oth)
            ],
            axis=1,
        )

    down_pieces = [piece((down_weight[0],), k) for k in range(4)]
    down_own = down_pieces[:1] + [shifted(down_pieces[k], k) for k in (1, 2, 3)]
    down_other = [swapped(w) for w in down_own]
    saved_own = jnp.concatenate([saved_gate[0].T, saved_up[0].T], axis=0)
    saved_all = jnp.concatenate([saved_own, swapped(saved_own)], axis=0)

    start = suffix_start[0]
    suffix_token = (token >= start) & (token < start + SUFFIX)
    ids = expert_ids.T
    match = ids[None] == jnp.arange(n_expert, dtype=jnp.int32)[:, None, None]
    share = gate_scores / jnp.sum(gate_scores, axis=1, keepdims=True)
    taken = jnp.sum(match.astype(jnp.float32), axis=1)
    share = jnp.sum(jnp.where(match, share.T[None], 0.0), axis=1)
    earlier = token[:, None] < token[None, :]
    same = suffix_token[:, None] == suffix_token[None, :]
    ahead = jnp.where(same, earlier, suffix_token[:, None])
    counts = taken.astype(jnp.bfloat16)
    place = dot(counts, ahead.astype(jnp.bfloat16), NN)
    place = jnp.where(taken > 0.5, place, -1.0).astype(jnp.int32)
    slot = dot(counts, earlier.astype(jnp.bfloat16), NN)
    chosen = place[:, None, :] == jnp.arange(PAD, dtype=jnp.int32)[None, :, None]
    weight = jnp.where(chosen, share[:, None, :], 0.0)
    weight_high = weight.astype(jnp.bfloat16)
    weight_low = (weight - weight_high.astype(jnp.float32)).astype(jnp.bfloat16)
    lane = jnp.arange(SLICE, dtype=jnp.int32)
    slot_of = jnp.sum(
        jnp.where(place[:, :, None] == lane[None, None, :128], slot[:, :, None], 0.0), axis=1
    )
    slot_of = jnp.pad(slot_of, ((0, 0), (0, SLICE - 128)))

    spread = chosen.astype(jnp.bfloat16).reshape(n_expert * PAD, seq_len)
    buffer = dot(spread, out_grad, NN).astype(jnp.bfloat16).reshape(n_expert, PAD, SLICE)
    last_row = jnp.arange(PAD, dtype=jnp.int32) == PAD - 1
    buffer = jnp.where(last_row[None, :, None], slot_of[:, None, :].astype(jnp.bfloat16), buffer)

    def exchanged(value):
        return lax.all_to_all(value, "expert", split_axis=0, concat_axis=0, tiled=True)

    arrived = exchanged(buffer)
    back_pieces = [piece((gate_weight[0].T, up_weight[0].T), k) for k in range(4)]
    back_own = back_pieces[:1] + [shifted(back_pieces[k], k) for k in (1, 2, 3)]
    here = lax.dynamic_slice_in_dim(arrived, half * c, half, 0)
    there = lax.dynamic_slice_in_dim(arrived, half * (1 - c), half, 0)
    slot_of = here[:, PAD - 1, :PAD].astype(jnp.int32)
    slot_of = slot_of + capacity * (
        half * c + jnp.arange(half, dtype=jnp.int32)[:, None]
    )

    partials, saved_here = [], []
    for at, n in CHUNKS:
        rows = half * n
        mine = here[:, at : at + n].reshape(rows, SLICE)
        other = swapped(there[:, at : at + n].reshape(rows, SLICE))
        if partials:
            mine, partials[0][0] = lax.optimization_barrier((mine, partials[0][0]))
        partials.append(list(act_partials(mine, other, down_own, down_other)))
        if not saved_here:
            slot_of, partials[0][0] = lax.optimization_barrier((slot_of, partials[0][0]))
        picks = (
            slot_of[:, at : at + n].reshape(rows, 1)
            == jnp.arange(slot_count, dtype=jnp.int32)[None, :]
        ).astype(jnp.bfloat16)
        saved_here.append(dot(picks, saved_all, NT).astype(jnp.bfloat16))
    parts = [[p[0]] + [shifted(p[k], -k) for k in (1, 2, 3)] for p in partials]
    parts[0][0], parts[1][0] = lax.optimization_barrier((parts[0][0], parts[1][0]))
    grads = []
    for p, s in zip(parts, saved_here):
        grads.append(tuple(gated(p, s)))
    back_own, _ = lax.optimization_barrier((back_own, grads[0]))
    back_other = [swapped(w) for w in back_own]
    ring = []
    for top, bottom in grads:
        up_top, down_bottom = shifted(top, 1), shifted(bottom, -1)
        up_bottom, down_top = shifted(bottom, 1), shifted(top, -1)
        ring.append((up_top, up_bottom, down_top, down_bottom))
    grads[0], grads[1] = lax.optimization_barrier((grads[0], grads[1]))

    def expert_grads(j):
        up_top, up_bottom, down_top, down_bottom = ring[j]
        far = shifted(up_top, 1), shifted(down_bottom, -1)
        acc_own, acc_oth = back_first(
            [grads[j], (up_top, up_bottom), (down_top, down_bottom)],
            [back_own[0], back_own[1], back_own[3]],
            [back_other[0], back_other[1], back_other[3]],
        )
        both, out_oth = back_last(core, *far, back_own[2], back_other[2], acc_own, acc_oth)
        both = lax.dynamic_update_slice_in_dim(both, swapped(out_oth), out_oth.shape[0] * (1 - c), 0)
        return both.reshape(n_expert, CHUNKS[j][1], SLICE)

    first_grads = expert_grads(0)

    tn = (((0,), (0,)), ((), ()))

    def combined(high, low, returned):
        return dot(high, returned, tn) + dot(low, returned, tn)

    def finished(grad, moe_grad, resid):
        scaled = moe_grad * norm_gain[None, :]
        sums = jnp.stack([jnp.sum(resid * resid, axis=1), jnp.sum(scaled * resid, axis=1)])
        sums = summed(sums)
        inverse = lax.rsqrt(sums[0] / D + 1e-06)
        factor = inverse * inverse * sums[1] / D
        return (
            grad.astype(jnp.float32) + inverse[:, None] * (scaled - resid * factor[:, None])
        ).astype(jnp.bfloat16)

    def flat(value, at, n):
        return value[:, at : at + n].reshape(n_expert * n, seq_len)

    first = CHUNKS[0][1]
    picked = jnp.arange(24, dtype=jnp.int32)
    picked = jnp.where(picked < SUFFIX, start + picked, -1)
    pick = (picked[:, None] == token[None, :]).astype(jnp.bfloat16)
    returned = exchanged(first_grads).reshape(n_expert * first, SLICE)
    suffix_high, suffix_low = (
        dot(flat(w, 0, first), pick, NT).astype(jnp.bfloat16) for w in (weight_high, weight_low)
    )
    suffix = finished(
        dot(pick, out_grad, NN),
        combined(suffix_high, suffix_low, returned),
        dot(pick, residual_stream, NN),
    )
    ring[1], grads[1], suffix = lax.optimization_barrier((ring[1], grads[1], suffix))
    suffix = exchanged(jnp.broadcast_to(suffix[None], (n_expert, 24, SLICE)))
    rest = exchanged(expert_grads(1)).reshape(n_expert * CHUNKS[1][1], SLICE)
    top, bottom = (
        suffix[at : at + half, :SUFFIX].reshape(half * SUFFIX, SLICE) for at in (0, half)
    )
    up_top, down_bottom = shifted(top, 1), shifted(bottom, -1)
    up_bottom, down_top = shifted(bottom, 1), shifted(top, -1)
    other = [swapped(part) for part in (top, bottom)]
    far = shifted(up_top, 1), shifted(down_bottom, -1)
    prev, succ = (up_top, up_bottom), (down_top, down_bottom)
    prev_x = [swapped(part) for part in prev]
    succ_x = [swapped(part) for part in succ]

    def of(k, core):
        return (y + k) % 4 * 2 + core

    at = jnp.stack([of(0, c), of(0, 1 - c), of(3, c), of(1, c), of(3, 1 - c), of(1, 1 - c)])
    acc = score_first(
        [(top, bottom), other, prev, succ, prev_x, succ_x], at.astype(jnp.int32), embedding
    )
    far, acc = lax.optimization_barrier((far, acc))
    far_x = [swapped(part) for part in far]
    rest, _ = lax.optimization_barrier((rest, (up_top, down_bottom)))
    moe_grad = combined(flat(weight_high, 0, first), flat(weight_low, 0, first), returned)
    moe_grad = moe_grad + combined(
        flat(weight_high, *CHUNKS[1]), flat(weight_low, *CHUNKS[1]), rest
    )
    token_grad = finished(out_grad, moe_grad, residual_stream.astype(jnp.float32))

    at = jnp.stack([of(2, c), of(2, 1 - c)]).astype(jnp.int32)
    scores = score_last([far, far_x], at, embedding, acc, allowed)
    return (token_grad, scores)


def solution(mesh):
    placed = (
        P("expert", "vocab"),
        P("expert", "vocab"),
        P("vocab"),
        P("expert", None),
        P("expert", None),
        P("expert", None, "vocab"),
        P("expert", None, "vocab"),
        P("expert", None, "vocab"),
        P("expert", None, "vocab"),
        P("expert", "vocab", None),
        P(("expert", "vocab"), None),
        P(("expert", "vocab")),
        P("expert"),
    )

    return jax.shard_map(
        shards,
        mesh=mesh,
        in_specs=placed,
        out_specs=(P("expert", "vocab"), P(None, ("expert", "vocab"))),
        check_vma=False,
    )
```

```python
import functools

import jax
import jax.numpy as jnp
from jax import lax
from jax.experimental import pallas as pl
from jax.experimental.pallas import tpu as pltpu
from jax.sharding import PartitionSpec as P


D = 4096
SUFFIX = 20
PAD = 40
SLICE = 512
HID = 192
CHUNKS = ((0, 24), (24, 16))
TILE = 160
NT = (((1,), (1,)), ((), ()))
NN = (((1,), (0,)), ((), ()))


def shifted(value, by):
    n = lax.axis_size("vocab")
    return lax.ppermute(value, "vocab", [(i, (i + 2 * by) % n) for i in range(n)])


def swapped(value):
    n = lax.axis_size("vocab")
    return lax.ppermute(value, "vocab", [(i, i ^ 1) for i in range(n)])


def summed(value):
    n = lax.axis_size("vocab")
    parts = lax.all_to_all(
        jnp.broadcast_to(value[None], (n, *value.shape)), "vocab", 0, 0, tiled=True
    )
    return jnp.sum(parts, axis=0)


def dot(a, b, dims):
    return lax.dot_general(a, b, dims, preferred_element_type=jnp.float32)


def tiles(rows, width):
    return pl.BlockSpec((rows // 2, width), lambda i, *_: (i, 0))


def half_tiles(rows, width):
    return pl.BlockSpec((rows // 2, width), lambda i, core: (2 * core[0] + i, 0))


def const(shape, *index):
    return pl.BlockSpec(shape, lambda i, *_: index)


def params():
    return pltpu.CompilerParams(dimension_semantics=("arbitrary",))


def fetches(refs, buffers, sems):
    copies = [
        pltpu.make_async_copy(ref, buf, sems.at[j])
        for j, (ref, buf) in enumerate(zip(refs, buffers))
    ]
    first = pl.program_id(0) == 0

    def start():
        for copy in copies:
            copy.start()

    def wait(j):
        pl.when(first)(copies[j].wait)

    pl.when(first)(start)
    return wait


ANYWHERE = pl.BlockSpec(memory_space=pl.ANY)


def act_body(xo, xx, t0, t1, t2, t3, other, a0, a1, a2, a3, weights, sems):
    refs, buffers = [], []
    for k, t in enumerate((t0, t1, t2, t3)):
        refs += [t, other.at[pl.ds(k * HID, HID)]]
        buffers += [weights.at[2 * k], weights.at[2 * k + 1]]
    wait = fetches(refs, buffers, sems)
    mine, theirs = xo[...], xx[...]
    for k, a in enumerate((a0, a1, a2, a3)):
        t, s = weights.at[2 * k], weights.at[2 * k + 1]
        wait(2 * k)
        own = dot(mine, t[:, :SLICE], NT) + dot(theirs, t[:, SLICE:], NT)
        a[:, :HID] = own.astype(jnp.bfloat16)
        wait(2 * k + 1)
        oth = dot(mine, s[:, SLICE:], NT) + dot(theirs, s[:, :SLICE], NT)
        a[:, HID:] = oth.astype(jnp.bfloat16)


def act_partials(mine, other, own_w, other_w):
    rows = other.shape[0]
    return pl.pallas_call(
        act_body,
        grid=(2,),
        in_specs=[tiles(rows, SLICE)] * 2 + [ANYWHERE] * 5,
        out_specs=[tiles(rows, 2 * HID)] * 4,
        out_shape=[jax.ShapeDtypeStruct((rows, 2 * HID), jnp.bfloat16)] * 4,
        scratch_shapes=[
            pltpu.VMEM((8, HID, 2 * SLICE), jnp.bfloat16),
            pltpu.SemaphoreType.DMA((8,)),
        ],
        compiler_params=params(),
        cost_estimate=pl.CostEstimate(
            flops=2 * rows * 2 * SLICE * 8 * HID, bytes_accessed=6_000_000, transcendentals=0
        ),
        name="act_partials",
    )(mine, other, *own_w, other_w)


def gated_body(a0, a1, a2, a3, saved, top, bottom):
    act = (a0[...].astype(jnp.float32) + a1[...].astype(jnp.float32)) + (
        a2[...].astype(jnp.float32) + a3[...].astype(jnp.float32)
    )

    def store(out):
        for at in (0, 1):
            a = act[:, at * HID : (at + 1) * HID]
            base = 2 * at * HID
            g = saved[:, base : base + HID].astype(jnp.float32)
            u = saved[:, base + HID : base + 2 * HID].astype(jnp.float32)
            s = jax.nn.sigmoid(g)
            out[:, base : base + HID] = (a * u * s * (1.0 + g * (1.0 - s))).astype(jnp.bfloat16)
            out[:, base + HID : base + 2 * HID] = (a * g * s).astype(jnp.bfloat16)

    pl.when(pl.program_id(0) == 0)(lambda: store(top))
    pl.when(pl.program_id(0) == 1)(lambda: store(bottom))


def gated(parts, saved):
    rows = saved.shape[0]
    return pl.pallas_call(
        gated_body,
        grid=(2,),
        in_specs=[tiles(rows, 2 * HID)] * 4 + [tiles(rows, 4 * HID)],
        out_specs=[const((rows // 2, 4 * HID), 0, 0)] * 2,
        out_shape=[jax.ShapeDtypeStruct((rows // 2, 4 * HID), jnp.bfloat16)] * 2,
        compiler_params=params(),
        cost_estimate=pl.CostEstimate(
            flops=rows * 2 * HID * 20, bytes_accessed=3_000_000, transcendentals=rows * 2 * HID
        ),
        name="gated",
    )(*parts, saved)


def back_body(kept, *refs):
    n = len(kept)
    tops, bottoms, own_w = refs[:n], refs[n : 2 * n], refs[2 * n : 3 * n]
    other_w, out_own, out_oth, weights, sems = refs[3 * n :]
    sources, buffers = [], []
    for j, k in enumerate(kept):
        sources += [own_w[j], other_w.at[pl.ds(k * 2 * HID, 2 * HID)]]
        buffers += [weights.at[2 * j], weights.at[2 * j + 1]]
    wait = fetches(sources, buffers, sems)
    upper = pl.program_id(0) == 0
    own = oth = None
    for j in range(n):
        b = jnp.where(upper, tops[j][...], bottoms[j][...])
        t, s = weights.at[2 * j], weights.at[2 * j + 1]
        left, right = b[:, : 2 * HID], b[:, 2 * HID :]
        wait(2 * j)
        o, x = dot(left, t[:, :SLICE], NN), dot(left, t[:, SLICE:], NN)
        own = o if own is None else own + o
        oth = x if oth is None else oth + x
        wait(2 * j + 1)
        own = own + dot(right, s[:, SLICE:], NN)
        oth = oth + dot(right, s[:, :SLICE], NN)
    out_own[...] = own
    out_oth[...] = oth


def back_first(blocks, kept, own_w, other_w):
    rows, n = 2 * blocks[0][0].shape[0], len(blocks)
    return pl.pallas_call(
        functools.partial(back_body, kept),
        grid=(2,),
        in_specs=[const((rows // 2, 4 * HID), 0, 0)] * (2 * n) + [ANYWHERE] * (n + 1),
        out_specs=[tiles(rows, SLICE)] * 2,
        out_shape=[jax.ShapeDtypeStruct((rows, SLICE), jnp.float32)] * 2,
        scratch_shapes=[
            pltpu.VMEM((2 * n, 2 * HID, 2 * SLICE), jnp.bfloat16),
            pltpu.SemaphoreType.DMA((2 * n,)),
        ],
        compiler_params=params(),
        cost_estimate=pl.CostEstimate(
            flops=2 * rows * 2 * SLICE * 4 * HID * n, bytes_accessed=9_000_000, transcendentals=0
        ),
        name="back_first",
    )(*[b[0] for b in blocks], *[b[1] for b in blocks], *[own_w[k] for k in kept], other_w)


def last_body(core, top, bottom, own_w, other_w, acc_own, acc_oth, *refs):
    out_own, out_oth, weights, sems = refs
    source = other_w.at[pl.ds(2 * 2 * HID, 2 * HID)]
    wait = fetches((own_w, source), (weights.at[0], weights.at[1]), sems)
    b = jnp.where(pl.program_id(0) == 0, top[...], bottom[...])
    left, right = b[:, : 2 * HID], b[:, 2 * HID :]
    t, s = weights.at[0], weights.at[1]
    wait(0)
    own = acc_own[...] + dot(left, t[:, :SLICE], NN)
    oth = acc_oth[...] + dot(left, t[:, SLICE:], NN)
    wait(1)
    own = own + dot(right, s[:, SLICE:], NN)
    oth = oth + dot(right, s[:, :SLICE], NN)
    out_own[...] = own.astype(jnp.bfloat16)
    out_oth[...] = oth.astype(jnp.bfloat16)


def back_last(core, top, bottom, own_w, other_w, acc_own, acc_oth):
    rows = acc_own.shape[0]
    return pl.pallas_call(
        last_body,
        grid_spec=pltpu.PrefetchScalarGridSpec(
            num_scalar_prefetch=1,
            grid=(2,),
            in_specs=[const((rows // 2, 4 * HID), 0, 0)] * 2
            + [ANYWHERE] * 2
            + [tiles(rows, SLICE)] * 2,
            out_specs=[half_tiles(rows, SLICE), tiles(rows, SLICE)],
            scratch_shapes=[
                pltpu.VMEM((2, 2 * HID, 2 * SLICE), jnp.bfloat16),
                pltpu.SemaphoreType.DMA((2,)),
            ],
        ),
        out_shape=[
            jax.ShapeDtypeStruct((2 * rows, SLICE), jnp.bfloat16),
            jax.ShapeDtypeStruct((rows, SLICE), jnp.bfloat16),
        ],
        compiler_params=params(),
        cost_estimate=pl.CostEstimate(
            flops=2 * rows * 2 * SLICE * 4 * HID, bytes_accessed=5_000_000, transcendentals=0
        ),
        name="back_last",
    )(core, top, bottom, own_w, other_w, acc_own, acc_oth)


def score_body(n, half, at, *refs):
    blocks, tables, rest, out = refs[: 2 * n], refs[2 * n : 3 * n], refs[3 * n : -1], refs[-1]
    upper = pl.program_id(0) < half
    total = rest[0][...] if rest else None
    for j in range(n):
        one = dot(jnp.where(upper, blocks[2 * j][...], blocks[2 * j + 1][...]), tables[j][...], NT)
        total = one if total is None else total + one
    if len(rest) == 2:
        total = jnp.where(rest[1][...] > 0, -total, 0.0)
    out[...] = total


def scored(at, blocks, owners, table, acc=None, allowed=None):
    n, rows, words = len(blocks), 2 * blocks[0][0].shape[0], table.shape[0]
    half = rows // TILE // 2
    top = pl.BlockSpec((TILE, SLICE), lambda i, at: (jnp.minimum(i, half - 1), 0))
    bottom = pl.BlockSpec((TILE, SLICE), lambda i, at: (jnp.maximum(i - half, 0), 0))
    wide = pl.BlockSpec((TILE, words), lambda i, at: (i, 0))

    def slice_of(k, same):
        def index(i, at):
            y, c = lax.div(at[0], 2), lax.rem(at[0], 2)
            return (0, 2 * lax.rem(y + k, 4) + (c if same else 1 - c))

        return pl.BlockSpec((words, SLICE), index)

    specs = [top, bottom] * n + [slice_of(*owner) for owner in owners]
    operands = [part for b in blocks for part in b] + [table] * n
    if acc is not None:
        specs, operands = specs + [wide], operands + [acc]
    if allowed is not None:
        specs = specs + [pl.BlockSpec((1, words), lambda i, at: (0, 0))]
        operands = operands + [allowed.reshape(1, words)]
    return pl.pallas_call(
        functools.partial(score_body, n, half),
        grid_spec=pltpu.PrefetchScalarGridSpec(
            num_scalar_prefetch=1, grid=(rows // TILE,), in_specs=specs, out_specs=wide
        ),
        out_shape=jax.ShapeDtypeStruct((rows, words), jnp.float32),
        compiler_params=params(),
        cost_estimate=pl.CostEstimate(
            flops=2 * rows * words * SLICE * n, bytes_accessed=4_000_000, transcendentals=0
        ),
        name="scored",
    )(at, *operands)


def shards(
    out_grad,
    residual_stream,
    norm_gain,
    expert_ids,
    gate_scores,
    saved_gate,
    saved_up,
    gate_weight,
    up_weight,
    down_weight,
    embedding,
    allowed,
    suffix_start,
):
    n_expert = lax.axis_size("expert")
    seq_len = out_grad.shape[0]
    slot_count = saved_gate.shape[1]
    capacity = slot_count // n_expert
    v = lax.axis_index("vocab")
    y, c = v // 2, v % 2
    half = n_expert // 2

    core = c.astype(jnp.int32).reshape(1)
    token = jnp.arange(seq_len, dtype=jnp.int32)

    def piece(weights, k):
        to = (y + k) % 4 * (2 * SLICE)
        own, oth = to + c * SLICE, to + (1 - c) * SLICE
        return jnp.concatenate(
            [
                jnp.concatenate(
                    [lax.dynamic_slice_in_dim(w, at, SLICE, 1) for w in weights], axis=0
                )
                for at in (own, oth)
            ],
            axis=1,
        )

    down_pieces = [piece((down_weight[0],), k) for k in range(4)]
    down_own = down_pieces[:1] + [shifted(down_pieces[k], k) for k in (1, 2, 3)]
    down_other = swapped(jnp.concatenate(down_own, axis=0))
    saved_own = jnp.concatenate([saved_gate[0].T, saved_up[0].T], axis=0)
    saved_all = jnp.concatenate([saved_own, swapped(saved_own)], axis=0)

    start = suffix_start[0]
    suffix_token = (token >= start) & (token < start + SUFFIX)
    ids = expert_ids.T
    match = ids[None] == jnp.arange(n_expert, dtype=jnp.int32)[:, None, None]
    share = gate_scores / jnp.sum(gate_scores, axis=1, keepdims=True)
    taken = jnp.sum(match.astype(jnp.float32), axis=1)
    share = jnp.sum(jnp.where(match, share.T[None], 0.0), axis=1)
    earlier = token[:, None] < token[None, :]
    same = suffix_token[:, None] == suffix_token[None, :]
    ahead = jnp.where(same, earlier, suffix_token[:, None])
    counts = taken.astype(jnp.bfloat16)
    place = dot(counts, ahead.astype(jnp.bfloat16), NN)
    place = jnp.where(taken > 0.5, place, -1.0).astype(jnp.int32)
    slot = dot(counts, earlier.astype(jnp.bfloat16), NN)
    chosen = place[:, None, :] == jnp.arange(PAD, dtype=jnp.int32)[None, :, None]
    weight = jnp.where(chosen, share[:, None, :], 0.0)
    weight_high = weight.astype(jnp.bfloat16)
    weight_low = (weight - weight_high.astype(jnp.float32)).astype(jnp.bfloat16)
    lane = jnp.arange(SLICE, dtype=jnp.int32)
    slot_of = jnp.sum(
        jnp.where(place[:, :, None] == lane[None, None, :128], slot[:, :, None], 0.0), axis=1
    )
    slot_of = jnp.pad(slot_of, ((0, 0), (0, SLICE - 128)))

    spread = chosen.astype(jnp.bfloat16).reshape(n_expert * PAD, seq_len)
    buffer = dot(spread, out_grad, NN).astype(jnp.bfloat16).reshape(n_expert, PAD, SLICE)
    last_row = jnp.arange(PAD, dtype=jnp.int32) == PAD - 1
    buffer = jnp.where(last_row[None, :, None], slot_of[:, None, :].astype(jnp.bfloat16), buffer)

    def exchanged(value):
        return lax.all_to_all(value, "expert", split_axis=0, concat_axis=0, tiled=True)

    arrived = exchanged(buffer)
    back_pieces = [piece((gate_weight[0].T, up_weight[0].T), k) for k in range(4)]
    back_own = back_pieces[:1] + [shifted(back_pieces[k], k) for k in (1, 2, 3)]
    here = lax.dynamic_slice_in_dim(arrived, half * c, half, 0)
    there = lax.dynamic_slice_in_dim(arrived, half * (1 - c), half, 0)
    slot_of = here[:, PAD - 1, :PAD].astype(jnp.int32)
    slot_of = slot_of + capacity * (
        half * c + jnp.arange(half, dtype=jnp.int32)[:, None]
    )

    partials, saved_here = [], []
    for at, n in CHUNKS:
        rows = half * n
        mine = here[:, at : at + n].reshape(rows, SLICE)
        other = swapped(there[:, at : at + n].reshape(rows, SLICE))
        if partials:
            mine, partials[0][0] = lax.optimization_barrier((mine, partials[0][0]))
        partials.append(list(act_partials(mine, other, down_own, down_other)))
        if not saved_here:
            slot_of, partials[0][0] = lax.optimization_barrier((slot_of, partials[0][0]))
        picks = (
            slot_of[:, at : at + n].reshape(rows, 1)
            == jnp.arange(slot_count, dtype=jnp.int32)[None, :]
        ).astype(jnp.bfloat16)
        saved_here.append(dot(picks, saved_all, NT).astype(jnp.bfloat16))
    parts = [[p[0]] + [shifted(p[k], -k) for k in (1, 2, 3)] for p in partials]
    back_own, saved_here[1], partials[1][0] = lax.optimization_barrier(
        (back_own, saved_here[1], partials[1][0])
    )
    parts[1][0] = partials[1][0]
    back_stack = jnp.concatenate(back_own, axis=0)
    parts[0][0], parts[1][0], saved_here[1], back_stack = lax.optimization_barrier(
        (parts[0][0], parts[1][0], saved_here[1], back_stack)
    )
    back_other = swapped(back_stack)
    grads = []
    for p, s in zip(parts, saved_here):
        grads.append(tuple(gated(p, s)))
    ring = []
    for top, bottom in grads:
        up_top, down_bottom = shifted(top, 1), shifted(bottom, -1)
        up_bottom, down_top = shifted(bottom, 1), shifted(top, -1)
        ring.append((up_top, up_bottom, down_top, down_bottom))

    def expert_grads(j):
        up_top, up_bottom, down_top, down_bottom = ring[j]
        far = shifted(up_top, 1), shifted(down_bottom, -1)
        acc_own, acc_oth = back_first(
            [grads[j], (up_top, up_bottom), (down_top, down_bottom)], (0, 1, 3), back_own, back_other
        )
        both, out_oth = back_last(core, *far, back_own[2], back_other, acc_own, acc_oth)
        both = lax.dynamic_update_slice_in_dim(both, swapped(out_oth), out_oth.shape[0] * (1 - c), 0)
        return both.reshape(n_expert, CHUNKS[j][1], SLICE)

    first_grads = expert_grads(0)

    tn = (((0,), (0,)), ((), ()))

    def combined(high, low, returned):
        return dot(high, returned, tn) + dot(low, returned, tn)

    def finished(grad, moe_grad, resid):
        scaled = moe_grad * norm_gain[None, :]
        sums = jnp.stack([jnp.sum(resid * resid, axis=1), jnp.sum(scaled * resid, axis=1)])
        sums = summed(sums)
        inverse = lax.rsqrt(sums[0] / D + 1e-06)
        factor = inverse * inverse * sums[1] / D
        return (
            grad.astype(jnp.float32) + inverse[:, None] * (scaled - resid * factor[:, None])
        ).astype(jnp.bfloat16)

    def flat(value, at, n):
        return value[:, at : at + n].reshape(n_expert * n, seq_len)

    first = CHUNKS[0][1]
    picked = jnp.arange(24, dtype=jnp.int32)
    picked = jnp.where(picked < SUFFIX, start + picked, -1)
    pick = (picked[:, None] == token[None, :]).astype(jnp.bfloat16)
    returned = exchanged(first_grads).reshape(n_expert * first, SLICE)
    suffix_high, suffix_low = (
        dot(flat(w, 0, first), pick, NT).astype(jnp.bfloat16) for w in (weight_high, weight_low)
    )
    suffix = finished(
        dot(pick, out_grad, NN),
        combined(suffix_high, suffix_low, returned),
        dot(pick, residual_stream, NN),
    )
    ring[1], grads[1], suffix = lax.optimization_barrier((ring[1], grads[1], suffix))
    suffix = exchanged(jnp.broadcast_to(suffix[None], (n_expert, 24, SLICE)))
    rest = exchanged(expert_grads(1)).reshape(n_expert * CHUNKS[1][1], SLICE)
    top, bottom = (
        suffix[at : at + half, :SUFFIX].reshape(half * SUFFIX, SLICE) for at in (0, half)
    )
    up_top, down_bottom = shifted(top, 1), shifted(bottom, -1)
    up_bottom, down_top = shifted(bottom, 1), shifted(top, -1)
    other = [swapped(part) for part in (top, bottom)]
    far = shifted(up_top, 1), shifted(down_bottom, -1)
    prev, succ = (up_top, up_bottom), (down_top, down_bottom)
    prev_x = [swapped(part) for part in prev]
    succ_x = [swapped(part) for part in succ]

    at = v.astype(jnp.int32).reshape(1)
    acc = scored(at, [(top, bottom), other], ((0, True), (0, False)), embedding)
    acc = scored(
        at,
        [prev, succ, prev_x, succ_x],
        ((3, True), (1, True), (3, False), (1, False)),
        embedding,
        acc,
    )
    far, acc = lax.optimization_barrier((far, acc))
    far_x = [swapped(part) for part in far]
    rest, _ = lax.optimization_barrier((rest, (up_top, down_bottom)))
    moe_grad = combined(flat(weight_high, 0, first), flat(weight_low, 0, first), returned)
    moe_grad = moe_grad + combined(
        flat(weight_high, *CHUNKS[1]), flat(weight_low, *CHUNKS[1]), rest
    )
    token_grad = finished(out_grad, moe_grad, residual_stream.astype(jnp.float32))

    scores = scored(at, [far, far_x], ((2, True), (2, False)), embedding, acc, allowed)
    return (token_grad, scores)


def solution(mesh):
    placed = (
        P("expert", "vocab"),
        P("expert", "vocab"),
        P("vocab"),
        P("expert", None),
        P("expert", None),
        P("expert", None, "vocab"),
        P("expert", None, "vocab"),
        P("expert", None, "vocab"),
        P("expert", None, "vocab"),
        P("expert", "vocab", None),
        P(("expert", "vocab"), None),
        P(("expert", "vocab")),
        P("expert"),
    )

    return jax.shard_map(
        shards,
        mesh=mesh,
        in_specs=placed,
        out_specs=(P("expert", "vocab"), P(None, ("expert", "vocab"))),
        check_vma=False,
    )
```

```python
import functools

import jax
import jax.numpy as jnp
from jax import lax
from jax.experimental import pallas as pl
from jax.experimental.pallas import tpu as pltpu
from jax.sharding import PartitionSpec as P


D = 4096
SUFFIX = 20
PAD = 40
SLICE = 512
HID = 192
CHUNKS = ((0, 24), (24, 16))
TILE = 160
NT = (((1,), (1,)), ((), ()))
NN = (((1,), (0,)), ((), ()))


def shifted(value, by):
    n = lax.axis_size("vocab")
    return lax.ppermute(value, "vocab", [(i, (i + 2 * by) % n) for i in range(n)])


def swapped(value):
    n = lax.axis_size("vocab")
    return lax.ppermute(value, "vocab", [(i, i ^ 1) for i in range(n)])


def summed(value):
    n = lax.axis_size("vocab")
    parts = lax.all_to_all(
        jnp.broadcast_to(value[None], (n, *value.shape)), "vocab", 0, 0, tiled=True
    )
    return jnp.sum(parts, axis=0)


def dot(a, b, dims):
    return lax.dot_general(a, b, dims, preferred_element_type=jnp.float32)


def tiles(rows, width):
    return pl.BlockSpec((rows // 2, width), lambda i, *_: (i, 0))


def half_tiles(rows, width):
    return pl.BlockSpec((rows // 2, width), lambda i, core: (2 * core[0] + i, 0))


def const(shape, *index):
    return pl.BlockSpec(shape, lambda i, *_: index)


def params():
    return pltpu.CompilerParams(dimension_semantics=("arbitrary",))


def act_body(xo, xx, t0, t1, t2, t3, s0, s1, s2, s3, a0, a1, a2, a3):
    mine, other = xo[...], xx[...]
    for t, s, a in ((t0, s0, a0), (t1, s1, a1), (t2, s2, a2), (t3, s3, a3)):
        own = dot(mine, t[:, :SLICE], NT) + dot(other, t[:, SLICE:], NT)
        oth = dot(mine, s[:, SLICE:], NT) + dot(other, s[:, :SLICE], NT)
        a[:, :HID] = own.astype(jnp.bfloat16)
        a[:, HID:] = oth.astype(jnp.bfloat16)


def act_partials(mine, other, own_w, other_w):
    rows = other.shape[0]
    return pl.pallas_call(
        act_body,
        grid=(2,),
        in_specs=[tiles(rows, SLICE)] * 2 + [const((HID, 2 * SLICE), 0, 0)] * 8,
        out_specs=[tiles(rows, 2 * HID)] * 4,
        out_shape=[jax.ShapeDtypeStruct((rows, 2 * HID), jnp.bfloat16)] * 4,
        compiler_params=params(),
        cost_estimate=pl.CostEstimate(
            flops=2 * rows * 2 * SLICE * 8 * HID, bytes_accessed=6_000_000, transcendentals=0
        ),
        name="act_partials",
    )(mine, other, *own_w, *other_w)


def gated_body(a0, a1, a2, a3, saved, top, bottom):
    act = (a0[...].astype(jnp.float32) + a1[...].astype(jnp.float32)) + (
        a2[...].astype(jnp.float32) + a3[...].astype(jnp.float32)
    )

    def store(out):
        for at in (0, 1):
            a = act[:, at * HID : (at + 1) * HID]
            base = 2 * at * HID
            g = saved[:, base : base + HID].astype(jnp.float32)
            u = saved[:, base + HID : base + 2 * HID].astype(jnp.float32)
            s = jax.nn.sigmoid(g)
            out[:, base : base + HID] = (a * u * s * (1.0 + g * (1.0 - s))).astype(jnp.bfloat16)
            out[:, base + HID : base + 2 * HID] = (a * g * s).astype(jnp.bfloat16)

    pl.when(pl.program_id(0) == 0)(lambda: store(top))
    pl.when(pl.program_id(0) == 1)(lambda: store(bottom))


def gated(parts, saved):
    rows = saved.shape[0]
    return pl.pallas_call(
        gated_body,
        grid=(2,),
        in_specs=[tiles(rows, 2 * HID)] * 4 + [tiles(rows, 4 * HID)],
        out_specs=[const((rows // 2, 4 * HID), 0, 0)] * 2,
        out_shape=[jax.ShapeDtypeStruct((rows // 2, 4 * HID), jnp.bfloat16)] * 2,
        compiler_params=params(),
        cost_estimate=pl.CostEstimate(
            flops=rows * 2 * HID * 20, bytes_accessed=3_000_000, transcendentals=rows * 2 * HID
        ),
        name="gated",
    )(*parts, saved)


def back_body(n, *refs):
    tops, bottoms = refs[:n], refs[n : 2 * n]
    own_w, other_w = refs[2 * n : 3 * n], refs[3 * n : 4 * n]
    out_own, out_oth = refs[4 * n :]
    upper = pl.program_id(0) == 0
    own = oth = None
    for top, bottom, t, s in zip(tops, bottoms, own_w, other_w):
        b = jnp.where(upper, top[...], bottom[...])
        left, right = b[:, : 2 * HID], b[:, 2 * HID :]
        o = dot(left, t[:, :SLICE], NN) + dot(right, s[:, SLICE:], NN)
        x = dot(left, t[:, SLICE:], NN) + dot(right, s[:, :SLICE], NN)
        own = o if own is None else own + o
        oth = x if oth is None else oth + x
    out_own[...] = own
    out_oth[...] = oth


def back_first(blocks, own_w, other_w):
    rows, n = 2 * blocks[0][0].shape[0], len(blocks)
    return pl.pallas_call(
        functools.partial(back_body, n),
        grid=(2,),
        in_specs=[const((rows // 2, 4 * HID), 0, 0)] * (2 * n)
        + [const((2 * HID, 2 * SLICE), 0, 0)] * (2 * n),
        out_specs=[tiles(rows, SLICE)] * 2,
        out_shape=[jax.ShapeDtypeStruct((rows, SLICE), jnp.float32)] * 2,
        compiler_params=params(),
        cost_estimate=pl.CostEstimate(
            flops=2 * rows * 2 * SLICE * 4 * HID * n, bytes_accessed=9_000_000, transcendentals=0
        ),
        name="back_first",
    )(*[b[0] for b in blocks], *[b[1] for b in blocks], *own_w, *other_w)


def last_body(core, top, bottom, t, s, acc_own, acc_oth, out_own, out_oth):
    b = jnp.where(pl.program_id(0) == 0, top[...], bottom[...])
    left, right = b[:, : 2 * HID], b[:, 2 * HID :]
    own = acc_own[...] + dot(left, t[:, :SLICE], NN) + dot(right, s[:, SLICE:], NN)
    oth = acc_oth[...] + dot(left, t[:, SLICE:], NN) + dot(right, s[:, :SLICE], NN)
    out_own[...] = own.astype(jnp.bfloat16)
    out_oth[...] = oth.astype(jnp.bfloat16)


def back_last(core, top, bottom, t, s, acc_own, acc_oth):
    rows = acc_own.shape[0]
    return pl.pallas_call(
        last_body,
        grid_spec=pltpu.PrefetchScalarGridSpec(
            num_scalar_prefetch=1,
            grid=(2,),
            in_specs=[const((rows // 2, 4 * HID), 0, 0)] * 2
            + [const((2 * HID, 2 * SLICE), 0, 0)] * 2
            + [tiles(rows, SLICE)] * 2,
            out_specs=[half_tiles(rows, SLICE), tiles(rows, SLICE)],
        ),
        out_shape=[
            jax.ShapeDtypeStruct((2 * rows, SLICE), jnp.bfloat16),
            jax.ShapeDtypeStruct((rows, SLICE), jnp.bfloat16),
        ],
        compiler_params=params(),
        cost_estimate=pl.CostEstimate(
            flops=2 * rows * 2 * SLICE * 4 * HID, bytes_accessed=5_000_000, transcendentals=0
        ),
        name="back_last",
    )(core, top, bottom, t, s, acc_own, acc_oth)


def score_body(n, half, at, *refs):
    blocks, tables, rest, out = refs[: 2 * n], refs[2 * n : 3 * n], refs[3 * n : -1], refs[-1]
    upper = pl.program_id(0) < half
    total = rest[0][...] if rest else None
    for j in range(n):
        one = dot(jnp.where(upper, blocks[2 * j][...], blocks[2 * j + 1][...]), tables[j][...], NT)
        total = one if total is None else total + one
    if len(rest) == 2:
        total = jnp.where(rest[1][...] > 0, -total, 0.0)
    out[...] = total


def scored(at, blocks, owners, table, acc=None, allowed=None):
    n, rows, words = len(blocks), 2 * blocks[0][0].shape[0], table.shape[0]
    half = rows // TILE // 2
    top = pl.BlockSpec((TILE, SLICE), lambda i, at: (jnp.minimum(i, half - 1), 0))
    bottom = pl.BlockSpec((TILE, SLICE), lambda i, at: (jnp.maximum(i - half, 0), 0))
    wide = pl.BlockSpec((TILE, words), lambda i, at: (i, 0))

    def slice_of(k, same):
        def index(i, at):
            y, c = lax.div(at[0], 2), lax.rem(at[0], 2)
            return (0, 2 * lax.rem(y + k, 4) + (c if same else 1 - c))

        return pl.BlockSpec((words, SLICE), index)

    specs = [top, bottom] * n + [slice_of(*owner) for owner in owners]
    operands = [part for b in blocks for part in b] + [table] * n
    if acc is not None:
        specs, operands = specs + [wide], operands + [acc]
    if allowed is not None:
        specs = specs + [pl.BlockSpec((1, words), lambda i, at: (0, 0))]
        operands = operands + [allowed.reshape(1, words)]
    return pl.pallas_call(
        functools.partial(score_body, n, half),
        grid_spec=pltpu.PrefetchScalarGridSpec(
            num_scalar_prefetch=1, grid=(rows // TILE,), in_specs=specs, out_specs=wide
        ),
        out_shape=jax.ShapeDtypeStruct((rows, words), jnp.float32),
        compiler_params=params(),
        cost_estimate=pl.CostEstimate(
            flops=2 * rows * words * SLICE * n, bytes_accessed=4_000_000, transcendentals=0
        ),
        name="scored",
    )(at, *operands)


def shards(
    out_grad,
    residual_stream,
    norm_gain,
    expert_ids,
    gate_scores,
    saved_gate,
    saved_up,
    gate_weight,
    up_weight,
    down_weight,
    embedding,
    allowed,
    suffix_start,
):
    n_expert = lax.axis_size("expert")
    seq_len = out_grad.shape[0]
    slot_count = saved_gate.shape[1]
    capacity = slot_count // n_expert
    v = lax.axis_index("vocab")
    y, c = v // 2, v % 2
    half = n_expert // 2

    core = c.astype(jnp.int32).reshape(1)
    token = jnp.arange(seq_len, dtype=jnp.int32)

    def piece(weights, k):
        to = (y + k) % 4 * (2 * SLICE)
        own, oth = to + c * SLICE, to + (1 - c) * SLICE
        return jnp.concatenate(
            [
                jnp.concatenate(
                    [lax.dynamic_slice_in_dim(w, at, SLICE, 1) for w in weights], axis=0
                )
                for at in (own, oth)
            ],
            axis=1,
        )

    down_pieces = [piece((down_weight[0],), k) for k in range(4)]
    down_own = down_pieces[:1] + [shifted(down_pieces[k], k) for k in (1, 2, 3)]
    down_other = [swapped(w) for w in down_own]
    saved_own = jnp.concatenate([saved_gate[0].T, saved_up[0].T], axis=0)
    saved_all = jnp.concatenate([saved_own, swapped(saved_own)], axis=0)

    start = suffix_start[0]
    suffix_token = (token >= start) & (token < start + SUFFIX)
    ids = expert_ids.T
    match = ids[None] == jnp.arange(n_expert, dtype=jnp.int32)[:, None, None]
    share = gate_scores / jnp.sum(gate_scores, axis=1, keepdims=True)
    taken = jnp.sum(match.astype(jnp.float32), axis=1)
    share = jnp.sum(jnp.where(match, share.T[None], 0.0), axis=1)
    earlier = token[:, None] < token[None, :]
    same = suffix_token[:, None] == suffix_token[None, :]
    ahead = jnp.where(same, earlier, suffix_token[:, None])
    counts = taken.astype(jnp.bfloat16)
    place = dot(counts, ahead.astype(jnp.bfloat16), NN)
    place = jnp.where(taken > 0.5, place, -1.0).astype(jnp.int32)
    slot = dot(counts, earlier.astype(jnp.bfloat16), NN)
    chosen = place[:, None, :] == jnp.arange(PAD, dtype=jnp.int32)[None, :, None]
    weight = jnp.where(chosen, share[:, None, :], 0.0)
    weight_high = weight.astype(jnp.bfloat16)
    weight_low = (weight - weight_high.astype(jnp.float32)).astype(jnp.bfloat16)
    lane = jnp.arange(SLICE, dtype=jnp.int32)
    slot_of = jnp.sum(
        jnp.where(place[:, :, None] == lane[None, None, :128], slot[:, :, None], 0.0), axis=1
    )
    slot_of = jnp.pad(slot_of, ((0, 0), (0, SLICE - 128)))

    spread = chosen.astype(jnp.bfloat16).reshape(n_expert * PAD, seq_len)
    buffer = dot(spread, out_grad, NN).astype(jnp.bfloat16).reshape(n_expert, PAD, SLICE)
    last_row = jnp.arange(PAD, dtype=jnp.int32) == PAD - 1
    buffer = jnp.where(last_row[None, :, None], slot_of[:, None, :].astype(jnp.bfloat16), buffer)

    def exchanged(value):
        return lax.all_to_all(value, "expert", split_axis=0, concat_axis=0, tiled=True)

    arrived = exchanged(buffer)
    back_pieces = [piece((gate_weight[0].T, up_weight[0].T), k) for k in range(4)]
    back_own = back_pieces[:1] + [shifted(back_pieces[k], k) for k in (1, 2, 3)]
    here = lax.dynamic_slice_in_dim(arrived, half * c, half, 0)
    there = lax.dynamic_slice_in_dim(arrived, half * (1 - c), half, 0)
    slot_of = here[:, PAD - 1, :PAD].astype(jnp.int32)
    slot_of = slot_of + capacity * (
        half * c + jnp.arange(half, dtype=jnp.int32)[:, None]
    )

    partials, saved_here = [], []
    for at, n in CHUNKS:
        rows = half * n
        mine = here[:, at : at + n].reshape(rows, SLICE)
        other = swapped(there[:, at : at + n].reshape(rows, SLICE))
        if partials:
            mine, partials[0][0] = lax.optimization_barrier((mine, partials[0][0]))
        partials.append(list(act_partials(mine, other, down_own, down_other)))
        if not saved_here:
            slot_of, partials[0][0] = lax.optimization_barrier((slot_of, partials[0][0]))
        picks = (
            slot_of[:, at : at + n].reshape(rows, 1)
            == jnp.arange(slot_count, dtype=jnp.int32)[None, :]
        ).astype(jnp.bfloat16)
        saved_here.append(dot(picks, saved_all, NT).astype(jnp.bfloat16))
    parts = [[p[0]] + [shifted(p[k], -k) for k in (1, 2, 3)] for p in partials]
    parts[0][0], parts[1][0], saved_here[1] = lax.optimization_barrier(
        (parts[0][0], parts[1][0], saved_here[1])
    )
    grads = []
    for p, s in zip(parts, saved_here):
        grads.append(tuple(gated(p, s)))
    back_own, _ = lax.optimization_barrier((back_own, grads[0]))
    back_other = [swapped(w) for w in back_own]
    ring = []
    for top, bottom in grads:
        up_top, down_bottom = shifted(top, 1), shifted(bottom, -1)
        up_bottom, down_top = shifted(bottom, 1), shifted(top, -1)
        ring.append((up_top, up_bottom, down_top, down_bottom))

    def expert_grads(j):
        up_top, up_bottom, down_top, down_bottom = ring[j]
        far = shifted(up_top, 1), shifted(down_bottom, -1)
        acc_own, acc_oth = back_first(
            [grads[j], (up_top, up_bottom), (down_top, down_bottom)],
            [back_own[0], back_own[1], back_own[3]],
            [back_other[0], back_other[1], back_other[3]],
        )
        both, out_oth = back_last(core, *far, back_own[2], back_other[2], acc_own, acc_oth)
        both = lax.dynamic_update_slice_in_dim(both, swapped(out_oth), out_oth.shape[0] * (1 - c), 0)
        return both.reshape(n_expert, CHUNKS[j][1], SLICE)

    first_grads = expert_grads(0)

    tn = (((0,), (0,)), ((), ()))

    def combined(high, low, returned):
        return dot(high, returned, tn) + dot(low, returned, tn)

    def finished(grad, moe_grad, resid):
        scaled = moe_grad * norm_gain[None, :]
        sums = jnp.stack([jnp.sum(resid * resid, axis=1), jnp.sum(scaled * resid, axis=1)])
        sums = summed(sums)
        inverse = lax.rsqrt(sums[0] / D + 1e-06)
        factor = inverse * inverse * sums[1] / D
        return (
            grad.astype(jnp.float32) + inverse[:, None] * (scaled - resid * factor[:, None])
        ).astype(jnp.bfloat16)

    def flat(value, at, n):
        return value[:, at : at + n].reshape(n_expert * n, seq_len)

    first = CHUNKS[0][1]
    picked = jnp.arange(24, dtype=jnp.int32)
    picked = jnp.where(picked < SUFFIX, start + picked, -1)
    pick = (picked[:, None] == token[None, :]).astype(jnp.bfloat16)
    returned = exchanged(first_grads).reshape(n_expert * first, SLICE)
    suffix_high, suffix_low = (
        dot(flat(w, 0, first), pick, NT).astype(jnp.bfloat16) for w in (weight_high, weight_low)
    )
    suffix = finished(
        dot(pick, out_grad, NN),
        combined(suffix_high, suffix_low, returned),
        dot(pick, residual_stream, NN),
    )
    ring[1], grads[1], suffix = lax.optimization_barrier((ring[1], grads[1], suffix))
    suffix = exchanged(jnp.broadcast_to(suffix[None], (n_expert, 24, SLICE)))
    rest = exchanged(expert_grads(1)).reshape(n_expert * CHUNKS[1][1], SLICE)
    top, bottom = (
        suffix[at : at + half, :SUFFIX].reshape(half * SUFFIX, SLICE) for at in (0, half)
    )
    up_top, down_bottom = shifted(top, 1), shifted(bottom, -1)
    up_bottom, down_top = shifted(bottom, 1), shifted(top, -1)
    other = [swapped(part) for part in (top, bottom)]
    far = shifted(up_top, 1), shifted(down_bottom, -1)
    prev, succ = (up_top, up_bottom), (down_top, down_bottom)
    prev_x = [swapped(part) for part in prev]
    succ_x = [swapped(part) for part in succ]

    at = v.astype(jnp.int32).reshape(1)
    acc = scored(
        at,
        [(top, bottom), other, prev, succ, prev_x, succ_x],
        ((0, True), (0, False), (3, True), (1, True), (3, False), (1, False)),
        embedding,
    )
    far, acc = lax.optimization_barrier((far, acc))
    far_x = [swapped(part) for part in far]
    rest, _ = lax.optimization_barrier((rest, (up_top, down_bottom)))
    moe_grad = combined(flat(weight_high, 0, first), flat(weight_low, 0, first), returned)
    moe_grad = moe_grad + combined(
        flat(weight_high, *CHUNKS[1]), flat(weight_low, *CHUNKS[1]), rest
    )
    token_grad = finished(out_grad, moe_grad, residual_stream.astype(jnp.float32))

    scores = scored(at, [far, far_x], ((2, True), (2, False)), embedding, acc, allowed)
    return (token_grad, scores)


def solution(mesh):
    placed = (
        P("expert", "vocab"),
        P("expert", "vocab"),
        P("vocab"),
        P("expert", None),
        P("expert", None),
        P("expert", None, "vocab"),
        P("expert", None, "vocab"),
        P("expert", None, "vocab"),
        P("expert", None, "vocab"),
        P("expert", "vocab", None),
        P(("expert", "vocab"), None),
        P(("expert", "vocab")),
        P("expert"),
    )

    return jax.shard_map(
        shards,
        mesh=mesh,
        in_specs=placed,
        out_specs=(P("expert", "vocab"), P(None, ("expert", "vocab"))),
        check_vma=False,
    )
```
